32 devices in a mesh: dp: 4 (over y, x), ctx: 8 (over z, core).
Axes of the slice: x: 2, y: 2, z: 4, core: 2. Of those that a mesh axis runs over, the one named last changes fastest.
Arguments:
- inputs: bfloat16 [8, 1024, 1024], P('dp', 'ctx'), may hold values from -6 to 6
- prefix_len: int32 [8], P('dp'), may hold values from 102 to 512
- gain_attn: bfloat16 [1024], P(('dp', 'ctx')), may hold values from 0.25 to 1.75
- w_query: bfloat16 [1024, 2048], P(('dp', 'ctx')), may hold values from -0.1875 to 0.1875
- key_weight: bfloat16 [1024, 1024], P(('dp', 'ctx')), may hold values from -0.1875 to 0.1875
- value_weight: bfloat16 [1024, 1024], P(('dp', 'ctx')), may hold values from -0.1875 to 0.1875
- gain_query: bfloat16 [128], P(('dp', 'ctx')), may hold values from 1 to 2
- gain_key: bfloat16 [128], P(('dp', 'ctx')), may hold values from 1 to 2
- w_out: bfloat16 [2048, 1024], P(('dp', 'ctx')), may hold values from -3 to 3
- gain_mlp: bfloat16 [1024], P(('dp', 'ctx')), may hold values from 0.25 to 1.75
- w_gate: bfloat16 [1024, 3072], P(('dp', 'ctx')), may hold values from -0.1875 to 0.1875
- w_up: bfloat16 [1024, 3072], P(('dp', 'ctx')), may hold values from -0.1875 to 0.1875
- w_down: bfloat16 [3072, 1024], P(('dp', 'ctx')), may hold values from -0.109375 to 0.109375
- cotangent: bfloat16 [8, 1024, 1024], P('dp', 'ctx'), may hold values from -6 to 6
Outputs:
- output: bfloat16 [8, 1024, 1024], P('dp', 'ctx')
- input_grad: float32 [8, 1024, 1024], P('dp', 'ctx')
- grad_gain_attn: float32 [1024], P(('dp', 'ctx'))
- grad_w_query: float32 [1024, 2048], P(('dp', 'ctx'))
- grad_w_key: float32 [1024, 1024], P(('dp', 'ctx'))
- grad_w_value: float32 [1024, 1024], P(('dp', 'ctx'))
- grad_gain_query: float32 [128], P(('dp', 'ctx'))
- grad_gain_key: float32 [128], P(('dp', 'ctx'))
- grad_w_out: float32 [2048, 1024], P(('dp', 'ctx'))
- grad_gain_mlp: float32 [1024], P(('dp', 'ctx'))
- grad_w_gate: float32 [1024, 3072], P(('dp', 'ctx'))
- grad_w_up: float32 [1024, 3072], P(('dp', 'ctx'))
- grad_w_down: float32 [3072, 1024], P(('dp', 'ctx'))
The draws below stay inside these ranges and needn't reach their ends.
Inputs may be any that keep to these rules, and one draw needn't show every extreme that they name: `prefix_len`: prefix length of each sequence, in tokens.
All inputs are finite; a program needn't handle non-finite values.
Results may differ from the reference program's by a relative error of at most 0.02.
Values may be sent and summed in bfloat16 or wider, within the bound.
No kernel may reach another device: no remote copies, remote signals or barrier semaphores. Data moves between devices by JAX's collectives and lax.ppermute only.
A program may use at most 192 MiB of HBM per device.

```python
import math
import jax
import jax.numpy as jnp
from jax import lax

MODEL_WIDTH = 1024
QUERY_HEADS = 16
KEY_VALUE_HEADS = 8
HEAD_SIZE = 128
FF = 3072
LEN = 1024
NSEQ = 8


def touch_ends(array, key, least, top_value):
    index_at = [jax.random.randint(jax.random.fold_in(key, axis), (), 0, length) for axis, length in enumerate(array.shape)]
    longest = array.shape.index(max(array.shape))
    next_to = index_at[:longest] + [(index_at[longest] + 1) % array.shape[longest]] + index_at[longest + 1:]
    return array.at[tuple(index_at)].set(least).at[tuple(next_to)].set(top_value)


def levels(stream_key, shape, cuts, low, high):
    level = 1.0
    for position, parts in cuts:
        heights = jax.random.uniform(jax.random.fold_in(jax.random.fold_in(stream_key, 6), position), (parts,), jnp.float32, low / len(cuts), high / len(cuts))
        level = level * jnp.repeat(jnp.exp(heights), shape[position] // parts).reshape((-1,) + (1,) * (len(shape) - 1 - position))
    return level


def scatter_about(stream_key, extent, deviation, reach, shards=(), kind=jnp.bfloat16):
    level = levels(stream_key, extent, shards, -0.22, 0.18) if shards else 1.0
    drawn = jax.random.normal(stream_key, extent, jnp.float32) * deviation * level
    return jnp.minimum(jnp.maximum(drawn, -reach), reach).astype(kind)


def setup_inputs(seed: int = 0) -> dict:
    streams_of = jax.random.split(jax.random.key(seed), 15)
    inputs = scatter_about(streams_of[0], (NSEQ, LEN, MODEL_WIDTH), 1.0, 6.0, ((0, 4), (1, 8)))
    prefix_len = touch_ends(jax.random.randint(streams_of[1], (NSEQ,), LEN // 10, LEN // 2 + 1), jax.random.fold_in(streams_of[1], 1), LEN // 10, (LEN // 2 + 1) - 1).astype(jnp.int32)
    gain_attn = jnp.clip(1.0 + 0.15 * jax.random.normal(streams_of[2], (MODEL_WIDTH,), jnp.float32), 0.25, 1.75).astype(jnp.bfloat16)
    w_query = scatter_about(streams_of[3], (MODEL_WIDTH, QUERY_HEADS * HEAD_SIZE), MODEL_WIDTH ** -0.5, 0.1875, ((0, 32),))
    key_weight = scatter_about(streams_of[4], (MODEL_WIDTH, KEY_VALUE_HEADS * HEAD_SIZE), MODEL_WIDTH ** -0.5, 0.1875, ((0, 32),))
    value_weight = scatter_about(streams_of[5], (MODEL_WIDTH, KEY_VALUE_HEADS * HEAD_SIZE), MODEL_WIDTH ** -0.5, 0.1875, ((0, 32),))
    gain_query = jnp.clip(1.0 + 1.0 * jax.random.uniform(streams_of[6], (HEAD_SIZE,), jnp.float32) ** levels(streams_of[6], (HEAD_SIZE,), ((0, 32),), -0.2, 0.2), 1.0, 2.0).astype(jnp.bfloat16)
    gain_key = jnp.clip(1.0 + 1.0 * jax.random.uniform(streams_of[7], (HEAD_SIZE,), jnp.float32) ** levels(streams_of[7], (HEAD_SIZE,), ((0, 32),), -0.2, 0.2), 1.0, 2.0).astype(jnp.bfloat16)
    w_out = scatter_about(streams_of[8], (QUERY_HEADS * HEAD_SIZE, MODEL_WIDTH), (max(1, QUERY_HEADS * HEAD_SIZE * 2 // LEN)) ** -0.5, 3.0, ((0, 32),))
    gain_mlp = jnp.clip(1.0 + 0.15 * jax.random.normal(streams_of[9], (MODEL_WIDTH,), jnp.float32), 0.25, 1.75).astype(jnp.bfloat16)
    w_gate = scatter_about(streams_of[10], (MODEL_WIDTH, FF), MODEL_WIDTH ** -0.5, 0.1875, ((0, 32),))
    w_up = scatter_about(streams_of[11], (MODEL_WIDTH, FF), MODEL_WIDTH ** -0.5, 0.1875, ((0, 32),))
    w_down = scatter_about(streams_of[12], (FF, MODEL_WIDTH), FF ** -0.5, 0.109375, ((0, 32),))
    cotangent = scatter_about(streams_of[13], (NSEQ, LEN, MODEL_WIDTH), 1.0, 6.0, ((0, 4), (1, 8)))
    return {"inputs": inputs, "prefix_len": prefix_len, "gain_attn": gain_attn, "w_query": w_query, "key_weight": key_weight, "value_weight": value_weight, "gain_query": gain_query, "gain_key": gain_key, "w_out": w_out, "gain_mlp": gain_mlp, "w_gate": w_gate, "w_up": w_up, "w_down": w_down, "cotangent": cotangent}


EPSILON = 1e-06
THETA = 1000000.0
NEGATIVE = -1e+30

@jax.custom_vjp
def low(v):
    return lax.optimization_barrier(v.astype(jnp.bfloat16)).astype(jnp.float32)

@jax.custom_vjp
def low_back(v):
    return v

def low_keep(v):
    return (low(v), None)

def low_pass(kept, grad):
    return (grad,)

def back_keep(v):
    return (v, None)

def back_low(kept, grad):
    return (low(grad),)
low.defvjp(low_keep, low_pass)
low_back.defvjp(back_keep, back_low)

def multiplier(left, right):
    return jnp.dot(left, right, precision=lax.Precision.HIGHEST, preferred_element_type=jnp.float32)

def rope_tables(positions, width):
    half = width // 2
    freqs = THETA ** (-(jnp.arange(half).astype(jnp.float32) * 2.0) / width)
    angles = positions.astype(jnp.float32)[:, None] * freqs[None, :]
    cosine = jnp.concatenate([jnp.cos(angles), jnp.cos(angles)], axis=-1)
    sine = jnp.concatenate([jnp.sin(angles), jnp.sin(angles)], axis=-1)
    return (cosine, sine)

def rotate_half(value_rows):
    half = value_rows.shape[-1] // 2
    return jnp.concatenate([-value_rows[..., half:], value_rows[..., :half]], axis=-1)

def rms_norm(value_rows, gain):
    return value_rows * lax.rsqrt(lax.optimization_barrier(jnp.mean(value_rows * value_rows, axis=-1, keepdims=True)) + EPSILON) * gain

def block(xfloat, prefix, weights):
    gain_attn, w_query, key_weight, value_weight, gain_query, gain_key, w_out, gain_mlp, w_gate, w_up, w_down = weights
    token_length = xfloat.shape[0]
    head_group = QUERY_HEADS // KEY_VALUE_HEADS
    normalized_input = low(rms_norm(xfloat, gain_attn))
    query_raw = low_back(multiplier(normalized_input, w_query)).reshape(token_length, QUERY_HEADS, HEAD_SIZE)
    key_unnormed = low_back(multiplier(normalized_input, key_weight)).reshape(token_length, KEY_VALUE_HEADS, HEAD_SIZE)
    value_rows = low_back(low(multiplier(normalized_input, value_weight))).reshape(token_length, KEY_VALUE_HEADS, HEAD_SIZE)
    positions = jnp.arange(token_length, dtype=jnp.int32)
    cosine, sine = rope_tables(positions, HEAD_SIZE)
    cosine = cosine[:, None, :]
    sine = sine[:, None, :]
    query_normed = rms_norm(query_raw, gain_query)
    key_normed = rms_norm(key_unnormed, gain_key)
    query_rows = low(query_normed * cosine + rotate_half(query_normed) * sine)
    keys = low(key_normed * cosine + rotate_half(key_normed) * sine)
    query_head_groups = query_rows.reshape(token_length, KEY_VALUE_HEADS, head_group, HEAD_SIZE).transpose(1, 2, 0, 3)
    key_groups = keys.transpose(1, 0, 2)
    value_groups = value_rows.transpose(1, 0, 2)
    allowed = (positions[None, :] <= positions[:, None]) | (positions[None, :] < prefix)
    root = math.sqrt(HEAD_SIZE)

    def head_attention(operands):
        query_part, key_part, value_part = operands
        scores = low_back(jnp.einsum('gtd,jd->gtj', query_part, key_part, precision=lax.Precision.HIGHEST) / root)
        masked = jnp.where(allowed[None], scores, NEGATIVE)
        top = lax.optimization_barrier(jnp.max(masked, axis=-1, keepdims=True))
        expo = jnp.exp(masked - top)
        probs = expo / lax.optimization_barrier(jnp.sum(expo, axis=-1, keepdims=True))
        return jnp.einsum('gtj,jd->gtd', low(probs), value_part, precision=lax.Precision.HIGHEST)
    head_count = lax.map(jax.checkpoint(head_attention), (query_head_groups, key_groups, value_groups))
    attn = low_back(low(head_count.transpose(2, 0, 1, 3).reshape(token_length, QUERY_HEADS * HEAD_SIZE)))
    branch = low_back(multiplier(attn, w_out))
    resid = xfloat + branch
    mlp_in = low(rms_norm(resid, gain_mlp))
    gate = low_back(multiplier(mlp_in, w_gate))
    upper = low_back(multiplier(mlp_in, w_up))
    hidden = low(jax.nn.silu(gate) * upper)
    return resid + multiplier(hidden, w_down)

def reference(inputs, prefix_len, gain_attn, w_query, key_weight, value_weight, gain_query, gain_key, w_out, gain_mlp, w_gate, w_up, w_down, cotangent):
    weights = tuple((w.astype(jnp.float32) for w in (gain_attn, w_query, key_weight, value_weight, gain_query, gain_key, w_out, gain_mlp, w_gate, w_up, w_down)))
    zeros = tuple((jnp.zeros(w.shape, jnp.float32) for w in weights))

    def per_sequence(totals, items):
        seq_in, prefix, seq_cot = items

        def forward(xfloat, *params):
            return block(xfloat, prefix, params)
        result, pullback = jax.vjp(forward, seq_in.astype(jnp.float32), *weights)
        grads = pullback(seq_cot.astype(jnp.float32))
        totals = tuple((t + g for t, g in zip(totals, grads[1:])))
        return (totals, (result.astype(jnp.bfloat16), grads[0]))
    totals, (outputs, input_grads) = lax.scan(per_sequence, zeros, (inputs, prefix_len, cotangent))
    return (outputs, input_grads, totals[0], totals[1], totals[2], totals[3], totals[4], totals[5], totals[6], totals[7], totals[8], totals[9], totals[10])
```

```python
import functools
import math

import jax
import jax.numpy as jnp
from jax import lax
from jax.experimental import pallas as pl
from jax.experimental.pallas import tpu as pltpu
from jax.sharding import Mesh
from jax.sharding import PartitionSpec as P

QUERY_HEADS = 16
KEY_VALUE_HEADS = 8
HEAD_SIZE = 128
HEAD_GROUP = QUERY_HEADS // KEY_VALUE_HEADS
MAX_PREFIX = 512
BLOCK = 256

EPSILON = 1e-06
THETA = 1000000.0
NEGATIVE = -1e30
INV_ROOT = 1.0 / math.sqrt(HEAD_SIZE)

F32 = jnp.float32
BF16 = jnp.bfloat16


def dot_nn(left, right):
    return lax.dot_general(left, right, (((1,), (0,)), ((), ())), preferred_element_type=F32)


def dot_nt(left, right):
    return lax.dot_general(left, right, (((1,), (1,)), ((), ())), preferred_element_type=F32)


def dot_tn(left, right):
    return lax.dot_general(left, right, (((0,), (0,)), ((), ())), preferred_element_type=F32)


def rope_tables(length):
    half = HEAD_SIZE // 2
    freqs = THETA ** (-(jnp.arange(half).astype(F32) * 2.0) / HEAD_SIZE)
    angles = jnp.arange(length).astype(F32)[:, None] * freqs[None, :]
    cosine = jnp.concatenate([jnp.cos(angles), jnp.cos(angles)], axis=-1)
    sine = jnp.concatenate([-jnp.sin(angles), jnp.sin(angles)], axis=-1)
    return cosine, sine


def compiler_params(grid_dims):
    return pltpu.CompilerParams(
        dimension_semantics=("arbitrary",) * grid_dims, vmem_limit_bytes=56 * 1024 * 1024
    )


def whole_spec(shape):
    zeros = (0,) * len(shape)
    return pl.BlockSpec(shape, lambda *_: zeros)


def place_kernel(index_ref, *refs):
    *pieces, out = refs
    step = pl.program_id(0)
    for number, piece in enumerate(pieces):

        @pl.when(step == number)
        def _(piece=piece):
            out[...] = piece[...].reshape(out.shape)


def place(pieces, index):
    count = len(pieces)
    groups, rows, cols = pieces[0].shape
    return pl.pallas_call(
        place_kernel,
        out_shape=jax.ShapeDtypeStruct((groups, count, rows, cols), pieces[0].dtype),
        grid_spec=pltpu.PrefetchScalarGridSpec(
            num_scalar_prefetch=1,
            grid=(count,),
            in_specs=[pl.BlockSpec((groups, rows, cols), lambda i, s: (0, 0, 0))] * count,
            out_specs=pl.BlockSpec((groups, 1, rows, cols), lambda i, s: (0, s[i], 0, 0)),
        ),
        compiler_params=compiler_params(1),
        name="place",
    )(index, *pieces)


def qkv_kernel(
    x_ref, gain_ref, gq_ref, gk_ref, cos_ref, sin_ref, w_ref, normed_ref, raw_ref, q_ref, k_ref, v_ref,
    *, queries, keys,
):
    x = x_ref[...].astype(F32)
    scale = lax.rsqrt(jnp.mean(x * x, axis=-1, keepdims=True) + EPSILON)
    normed = (x * scale * gain_ref[...]).astype(BF16)
    normed_ref[...] = normed
    y = dot_nn(normed, w_ref[...])
    width = (queries + keys) * HEAD_SIZE
    raw_ref[...] = y[:, :width]
    v_ref[...] = y[:, width:].astype(BF16)
    cosine = cos_ref[...]
    sine = sin_ref[...]
    for head in range(queries + keys):
        u = y[:, head * HEAD_SIZE : (head + 1) * HEAD_SIZE]
        s = lax.rsqrt(jnp.mean(u * u, axis=-1, keepdims=True) + EPSILON)
        gain = gq_ref[...] if head < queries else gk_ref[...]
        un = u * s * gain
        rotated = (un * cosine + pltpu.roll(un, HEAD_SIZE // 2, 1) * sine).astype(BF16)
        if head < queries:
            q_ref[:, head * HEAD_SIZE : (head + 1) * HEAD_SIZE] = rotated
        else:
            at = (head - queries) * HEAD_SIZE
            k_ref[:, at : at + HEAD_SIZE] = rotated


def qkv_forward(x, gain, gain_query, gain_key, cosine, sine, weight, queries, keys):
    tokens, width = x.shape
    rows = lambda cols: pl.BlockSpec((BLOCK, cols), lambda i: (i, 0))
    total = (queries + 2 * keys) * HEAD_SIZE
    raw = (queries + keys) * HEAD_SIZE
    return pl.pallas_call(
        functools.partial(qkv_kernel, queries=queries, keys=keys),
        out_shape=(
            jax.ShapeDtypeStruct((tokens, width), BF16),
            jax.ShapeDtypeStruct((tokens, raw), F32),
            jax.ShapeDtypeStruct((tokens, queries * HEAD_SIZE), BF16),
            jax.ShapeDtypeStruct((tokens, keys * HEAD_SIZE), BF16),
            jax.ShapeDtypeStruct((tokens, keys * HEAD_SIZE), BF16),
        ),
        grid=(tokens // BLOCK,),
        in_specs=[
            rows(width),
            whole_spec((1, width)),
            whole_spec((1, HEAD_SIZE)),
            whole_spec((1, HEAD_SIZE)),
            rows(HEAD_SIZE),
            rows(HEAD_SIZE),
            pl.BlockSpec((width, total), lambda i: (0, 0)),
        ],
        out_specs=(
            rows(width),
            rows(raw),
            rows(queries * HEAD_SIZE),
            rows(keys * HEAD_SIZE),
            rows(keys * HEAD_SIZE),
        ),
        compiler_params=compiler_params(1),
        cost_estimate=pl.CostEstimate(
            flops=2 * tokens * width * total, bytes_accessed=14 * tokens * width, transcendentals=0
        ),
        name="qkv_forward",
    )(x, gain, gain_query, gain_key, cosine, sine, weight)


def masked_scores(k, q, prefix, start, length, long):
    scores = dot_nt(k, q) * INV_ROOT
    rows = q.shape[0]
    if long:
        free = scores[:MAX_PREFIX]
        later = scores[MAX_PREFIX:]
        key = lax.broadcasted_iota(jnp.int32, (length - MAX_PREFIX, rows), 0) + MAX_PREFIX
        token = lax.broadcasted_iota(jnp.int32, (length - MAX_PREFIX, rows), 1) + start
        return jnp.concatenate([free, jnp.where(key <= token, later, NEGATIVE)], axis=0)
    key = lax.broadcasted_iota(jnp.int32, (length, rows), 0)
    token = lax.broadcasted_iota(jnp.int32, (length, rows), 1) + start
    return jnp.where((key <= token) | (key < prefix), scores, NEGATIVE)


def attention_forward_kernel(
    prefix_ref, q_ref, k_ref, v_ref, w_ref, attn_ref, lse_ref, part_ref, acc_ref, *, tokens
):
    block = pl.program_id(0)
    group = pl.program_id(1)
    start = block * BLOCK
    prefix = prefix_ref[0]

    def body(length, long):
        k = k_ref[:length]
        v = v_ref[:length]
        for head in range(HEAD_GROUP):
            lanes = slice(head * HEAD_SIZE, (head + 1) * HEAD_SIZE)
            scores = masked_scores(k, q_ref[:, lanes], prefix, start, length, long)
            top = jnp.max(scores, axis=0, keepdims=True)
            expo = jnp.exp(scores - top)
            total = jnp.sum(expo, axis=0, keepdims=True)
            probs = (expo * (1.0 / total)).astype(BF16)
            attn_ref[:, lanes] = dot_tn(probs, v).astype(BF16)
            lse_ref[0, head : head + 1, :] = top + jnp.log(total)

    if tokens <= MAX_PREFIX:
        body(tokens, False)
    else:

        @pl.when(start < MAX_PREFIX)
        def _():
            body(MAX_PREFIX, False)

        @pl.when(start >= MAX_PREFIX)
        def _():
            body(tokens, True)

    part = dot_nn(attn_ref[...], w_ref[...])

    @pl.when(group == 0)
    def _():
        acc_ref[...] = part

    @pl.when(group > 0)
    def _():
        acc_ref[...] += part

    @pl.when(group == pl.num_programs(1) - 1)
    def _():
        part_ref[...] = acc_ref[...].astype(BF16)


def attention_forward(prefix, q, k, v, w_out):
    tokens = q.shape[0]
    groups = k.shape[1] // HEAD_SIZE
    width = w_out.shape[1]
    wide = HEAD_GROUP * HEAD_SIZE
    return pl.pallas_call(
        functools.partial(attention_forward_kernel, tokens=tokens),
        out_shape=(
            jax.ShapeDtypeStruct((tokens, groups * wide), BF16),
            jax.ShapeDtypeStruct((groups, 8, tokens), F32),
            jax.ShapeDtypeStruct((tokens, width), BF16),
        ),
        grid_spec=pltpu.PrefetchScalarGridSpec(
            num_scalar_prefetch=1,
            grid=(tokens // BLOCK, groups),
            in_specs=[
                pl.BlockSpec((BLOCK, wide), lambda i, g, s: (i, g)),
                pl.BlockSpec((tokens, HEAD_SIZE), lambda i, g, s: (0, g)),
                pl.BlockSpec((tokens, HEAD_SIZE), lambda i, g, s: (0, g)),
                pl.BlockSpec((wide, width), lambda i, g, s: (g, 0)),
            ],
            out_specs=(
                pl.BlockSpec((BLOCK, wide), lambda i, g, s: (i, g)),
                pl.BlockSpec((1, 8, BLOCK), lambda i, g, s: (g, 0, i)),
                pl.BlockSpec((BLOCK, width), lambda i, g, s: (i, 0)),
            ),
            scratch_shapes=[pltpu.VMEM((BLOCK, width), F32)],
        ),
        compiler_params=compiler_params(2),
        cost_estimate=pl.CostEstimate(
            flops=4 * tokens * tokens * groups * wide, bytes_accessed=8 * tokens * width,
            transcendentals=tokens * tokens * groups * HEAD_GROUP,
        ),
        name="attention_forward",
    )(prefix, q, k, v, w_out)


def mlp_kernel(x_ref, cot_ref, wgu_ref, wd_ref, hidden_ref, grad_ref, out_ref, back_ref, *, ff):
    both = dot_nn(x_ref[...], wgu_ref[...])
    gate = both[:, :ff]
    upper = both[:, ff:]
    sigma = jax.nn.sigmoid(gate)
    silu = gate * sigma
    hidden = (silu * upper).astype(BF16)
    hidden_ref[...] = hidden
    hidden_grad = dot_nt(cot_ref[...], wd_ref[...])
    gate_grad = (hidden_grad * upper * (sigma * (1.0 + gate * (1.0 - sigma)))).astype(BF16)
    up_grad = (hidden_grad * silu).astype(BF16)
    grad_ref[:, :ff] = gate_grad
    grad_ref[:, ff:] = up_grad
    back_ref[...] = dot_nt(grad_ref[...], wgu_ref[...]).astype(BF16)
    out_ref[...] = dot_nn(hidden, wd_ref[...]).astype(BF16)


def mlp(x, cot, w_gate_up, w_down):
    tokens, width = x.shape
    ff = w_down.shape[0]
    rows = lambda cols: pl.BlockSpec((BLOCK, cols), lambda i: (i, 0))
    return pl.pallas_call(
        functools.partial(mlp_kernel, ff=ff),
        out_shape=(
            jax.ShapeDtypeStruct((tokens, ff), BF16),
            jax.ShapeDtypeStruct((tokens, 2 * ff), BF16),
            jax.ShapeDtypeStruct((tokens, width), BF16),
            jax.ShapeDtypeStruct((tokens, width), BF16),
        ),
        grid=(tokens // BLOCK,),
        in_specs=[
            rows(width),
            rows(width),
            whole_spec((width, 2 * ff)),
            whole_spec((ff, width)),
        ],
        out_specs=(rows(ff), rows(2 * ff), rows(width), rows(width)),
        compiler_params=compiler_params(1),
        cost_estimate=pl.CostEstimate(
            flops=12 * tokens * width * ff, bytes_accessed=16 * tokens * width,
            transcendentals=tokens * ff,
        ),
        name="mlp",
    )(x, cot, w_gate_up, w_down)


def attention_backward_kernel(
    prefix_ref, og_ref, w_ref, q_ref, k_ref, v_ref, lse_ref, dq_ref, dk_ref, dv_ref, *, tokens
):
    block = pl.program_id(1)
    start = block * BLOCK
    prefix = prefix_ref[0]

    @pl.when(block == 0)
    def _():
        dk_ref[...] = jnp.zeros_like(dk_ref)
        dv_ref[...] = jnp.zeros_like(dv_ref)

    attn_grad = dot_nt(og_ref[...], w_ref[...]).astype(BF16)

    def body(length, long):
        k = k_ref[:length]
        v = v_ref[:length]
        for head in range(HEAD_GROUP):
            lanes = slice(head * HEAD_SIZE, (head + 1) * HEAD_SIZE)
            q = q_ref[:, lanes]
            grad = attn_grad[:, lanes]
            scores = masked_scores(k, q, prefix, start, length, long)
            probs = jnp.exp(scores - lse_ref[0, head : head + 1, :])
            probs_grad = dot_nt(v, grad)
            delta = jnp.sum(probs * probs_grad, axis=0, keepdims=True)
            score_grad = (probs * (probs_grad - delta)).astype(BF16)
            dq_ref[:, lanes] = dot_tn(score_grad, k) * INV_ROOT
            dk_ref[:length] += dot_nn(score_grad, q) * INV_ROOT
            dv_ref[:length] += dot_nn(probs.astype(BF16), grad)

    if tokens <= MAX_PREFIX:
        body(tokens, False)
    else:

        @pl.when(start < MAX_PREFIX)
        def _():
            body(MAX_PREFIX, False)

        @pl.when(start >= MAX_PREFIX)
        def _():
            body(tokens, True)


def attention_backward(prefix, out_grad, w_out, q, k, v, lse):
    tokens = q.shape[0]
    groups = k.shape[1] // HEAD_SIZE
    width = w_out.shape[1]
    wide = HEAD_GROUP * HEAD_SIZE
    return pl.pallas_call(
        functools.partial(attention_backward_kernel, tokens=tokens),
        out_shape=(
            jax.ShapeDtypeStruct((tokens, groups * wide), F32),
            jax.ShapeDtypeStruct((tokens, groups * HEAD_SIZE), F32),
            jax.ShapeDtypeStruct((tokens, groups * HEAD_SIZE), F32),
        ),
        grid_spec=pltpu.PrefetchScalarGridSpec(
            num_scalar_prefetch=1,
            grid=(groups, tokens // BLOCK),
            in_specs=[
                pl.BlockSpec((BLOCK, width), lambda g, i, s: (i, 0)),
                pl.BlockSpec((wide, width), lambda g, i, s: (g, 0)),
                pl.BlockSpec((BLOCK, wide), lambda g, i, s: (i, g)),
                pl.BlockSpec((tokens, HEAD_SIZE), lambda g, i, s: (0, g)),
                pl.BlockSpec((tokens, HEAD_SIZE), lambda g, i, s: (0, g)),
                pl.BlockSpec((1, 8, BLOCK), lambda g, i, s: (g, 0, i)),
            ],
            out_specs=(
                pl.BlockSpec((BLOCK, wide), lambda g, i, s: (i, g)),
                pl.BlockSpec((tokens, HEAD_SIZE), lambda g, i, s: (0, g)),
                pl.BlockSpec((tokens, HEAD_SIZE), lambda g, i, s: (0, g)),
            ),
        ),
        compiler_params=compiler_params(2),
        cost_estimate=pl.CostEstimate(
            flops=10 * tokens * tokens * groups * wide, bytes_accessed=16 * tokens * width,
            transcendentals=tokens * tokens * groups * HEAD_GROUP,
        ),
        name="attention_backward",
    )(prefix, out_grad, w_out, q, k, v, lse)


def qkv_backward_kernel(
    dq_ref, dk_ref, dv_ref, raw_ref, gq_ref, gk_ref, cos_ref, sin_ref, w_ref, grad_ref, back_ref, gain_ref,
    *, queries, keys,
):
    @pl.when(pl.program_id(0) == 0)
    def _():
        gain_ref[...] = jnp.zeros_like(gain_ref)

    cosine = cos_ref[...]
    sine = sin_ref[...]
    for head in range(queries + keys):
        lanes = slice(head * HEAD_SIZE, (head + 1) * HEAD_SIZE)
        is_query = head < queries
        at = (head - queries) * HEAD_SIZE
        w = dq_ref[:, lanes] if is_query else dk_ref[:, at : at + HEAD_SIZE]
        gain = gq_ref[...] if is_query else gk_ref[...]
        norm_grad = w * cosine - pltpu.roll(w, HEAD_SIZE // 2, 1) * sine
        u = raw_ref[:, lanes]
        s = lax.rsqrt(jnp.mean(u * u, axis=-1, keepdims=True) + EPSILON)
        weighted = gain * norm_grad
        inner = jnp.mean(weighted * u, axis=-1, keepdims=True)
        grad_ref[:, lanes] = (s * weighted - u * (s * s * s) * inner).astype(BF16)
        row = 0 if is_query else 1
        gain_ref[row : row + 1] += jnp.sum(norm_grad * u * s, axis=0, keepdims=True)
    width = (queries + keys) * HEAD_SIZE
    grad_ref[:, width:] = dv_ref[...].astype(BF16)
    back_ref[...] = dot_nt(grad_ref[...], w_ref[...]).astype(BF16)


def qkv_backward(dq, dk, dv, raw, gain_query, gain_key, cosine, sine, weight, queries, keys):
    tokens = dq.shape[0]
    width = weight.shape[0]
    total = (queries + 2 * keys) * HEAD_SIZE
    rows = lambda cols: pl.BlockSpec((BLOCK, cols), lambda i: (i, 0))
    return pl.pallas_call(
        functools.partial(qkv_backward_kernel, queries=queries, keys=keys),
        out_shape=(
            jax.ShapeDtypeStruct((tokens, total), BF16),
            jax.ShapeDtypeStruct((tokens, width), BF16),
            jax.ShapeDtypeStruct((8, HEAD_SIZE), F32),
        ),
        grid=(tokens // BLOCK,),
        in_specs=[
            rows(queries * HEAD_SIZE),
            rows(keys * HEAD_SIZE),
            rows(keys * HEAD_SIZE),
            rows((queries + keys) * HEAD_SIZE),
            whole_spec((1, HEAD_SIZE)),
            whole_spec((1, HEAD_SIZE)),
            rows(HEAD_SIZE),
            rows(HEAD_SIZE),
            pl.BlockSpec((width, total), lambda i: (0, 0)),
        ],
        out_specs=(rows(total), rows(width), whole_spec((8, HEAD_SIZE))),
        compiler_params=compiler_params(1),
        cost_estimate=pl.CostEstimate(
            flops=2 * tokens * width * total, bytes_accessed=14 * tokens * width, transcendentals=0
        ),
        name="qkv_backward",
    )(dq, dk, dv, raw, gain_query, gain_key, cosine, sine, weight)


def swap(value, axis):
    return lax.ppermute(value, axis, [(0, 1), (1, 0)])


def pick(value, index, axis=0):
    return lax.dynamic_index_in_dim(value, index, axis, keepdims=False)


def ordered(mine, other, bit):
    return jnp.where(bit == 0, jnp.stack([mine, other]), jnp.stack([other, mine]))


class Layout:
    def __init__(self):
        self.a, self.b, self.h, self.l, self.c = (lax.axis_index(n) for n in "abhlc")
        self.nb = lax.axis_size("b")
        self.nl = lax.axis_size("l")
        self.team = self.nl * 2
        self.teams = 4 * self.nb

    def team_index(self):
        l, c = self.l, self.c
        return jnp.stack([l * 2 + c, (1 - l) * 2 + c, l * 2 + 1 - c, (1 - l) * 2 + 1 - c])

    def plane_index(self):
        a, b = self.a, self.b
        return jnp.stack([a * 2 + b, a * 2 + 1 - b, (1 - a) * 2 + b, (1 - a) * 2 + 1 - b])

    def exchange(self, value):
        team, rows, cols = value.shape
        if self.nl != 2:
            return lax.all_to_all(value, ("l", "c"), 0, 0, tiled=True)
        value = value.reshape(2, 2, rows, cols)
        keep = pick(value, self.l)
        got = swap(pick(value, 1 - self.l), "l")
        both = jnp.stack([keep, got])
        kept = pick(both, self.c, 1)
        other = swap(pick(both, 1 - self.c, 1), "c")
        pieces = [kept[:1], kept[1:], other[:1], other[1:]]
        return place(pieces, self.team_index()).reshape(team, rows, cols)

    def team_gather(self, value):
        halves, span, width = value.shape
        if self.nl != 2:
            out = lax.all_gather(value, ("l", "c"), axis=1)
        else:
            far = swap(value, "l")
            near = swap(value, "c")
            corner = swap(far, "c")
            out = place([value, far, near, corner], self.team_index())
        return out.reshape(halves * self.team * span, width)

    def team_scatter(self, part, span):
        width = part.shape[1]
        part = part.reshape(2, self.nl, 2, span, width)
        if self.nl != 2:
            part = part.reshape(2, self.team, span, width)
            out = lax.psum_scatter(part, ("l", "c"), scatter_dimension=1, tiled=True)
            return out.reshape(2, span, width).astype(F32)
        got = swap(pick(part, 1 - self.c, 2), "c")
        both = pick(part, self.c, 2).astype(F32) + got.astype(F32)
        got = swap(pick(both, 1 - self.l, 1).astype(BF16), "l")
        return pick(both, self.l, 1) + got.astype(F32)

    def weight_gather(self, value):
        rows, cols = value.shape
        if self.nb != 2:
            return lax.all_gather(value, ("a", "b", "h"), axis=0)
        pair = ordered(value, swap(value, "h"), self.h).reshape(2 * rows, cols)
        over_b = swap(pair, "b")
        over_a = swap(pair, "a")
        corner = jnp.concatenate([swap(over_b[:rows], "a"), swap(over_a[rows:], "b")])
        pieces = [p[None] for p in (pair, over_b, over_a, corner)]
        return place(pieces, self.plane_index()).reshape(self.teams, rows, cols)

    def weight_scatter(self, part):
        teams, rows, cols = part.shape
        if self.nb != 2:
            part = part.astype(BF16)
            out = lax.psum_scatter(part, ("a", "b", "h"), scatter_dimension=0, tiled=True)
            return out.reshape(rows, cols).astype(F32)
        part = part.reshape(4, 2 * rows, cols)
        own, over_b, over_a, corner = (pick(part, i) for i in self.plane_index())
        corner = corner.astype(BF16)
        via_b = swap(corner[:rows], "b")
        via_a = swap(corner[rows:], "a")
        over_a = jnp.concatenate([over_a[:rows] + via_b.astype(F32), over_a[rows:]])
        over_b = jnp.concatenate([over_b[:rows], over_b[rows:] + via_a.astype(F32)])
        got_b = swap(over_b.astype(BF16), "b")
        got_a = swap(over_a.astype(BF16), "a")
        pair = (own + got_b.astype(F32) + got_a.astype(F32)).reshape(2, rows, cols)
        got = swap(pick(pair, 1 - self.h).astype(BF16), "h")
        return pick(pair, self.h) + got.astype(F32)


def norm_backward(rows, scale, gain, grad):
    weighted = gain * grad
    inner = jnp.mean(weighted * rows, axis=-1, keepdims=True)
    return scale * weighted - rows * (scale * scale * scale) * inner


def row_scale(rows):
    return lax.rsqrt(jnp.mean(rows * rows, axis=-1, keepdims=True) + EPSILON)


def per_device(
    inputs, prefix_len, gain_attn, w_query, key_weight, value_weight, gain_query, gain_key,
    w_out, gain_mlp, w_gate, w_up, w_down, cotangent,
):
    lay = Layout()
    team, teams = lay.team, lay.teams
    devices = team * teams
    span, width = inputs.shape[1:]
    tokens = 2 * team * span
    queries = QUERY_HEADS // team
    keys = KEY_VALUE_HEADS // team
    rows = w_query.shape[0]
    few = gain_query.shape[0]
    q_cols, k_cols = queries * HEAD_SIZE, keys * HEAD_SIZE
    qkv_cols = q_cols + 2 * k_cols
    out_rows, down_rows = w_out.shape[0], w_down.shape[0]
    ff = teams * down_rows

    def to_halves(value):
        return ordered(pick(value, lay.h), swap(pick(value, 1 - lay.h), "h"), lay.h)

    x_own = to_halves(inputs)
    x_all = lay.team_gather(x_own)
    prefix = pick(prefix_len, lay.h).reshape(1)

    extra = jnp.concatenate(
        [
            jnp.broadcast_to(gain_query[None, :], (rows, few)),
            jnp.broadcast_to(gain_key[None, :], (rows, few)),
            gain_attn[:, None],
            gain_mlp[:, None],
            jnp.zeros((rows, HEAD_SIZE - 2 * few - 2), BF16),
        ],
        axis=1,
    )
    split = lambda w: w.reshape(rows, team, -1)
    packed = jnp.concatenate(
        [
            split(w_query),
            split(key_weight),
            split(value_weight),
            jnp.broadcast_to(extra[:, None], (rows, team, HEAD_SIZE)),
        ],
        axis=2,
    ).transpose(1, 0, 2)
    packed = lay.exchange(packed).reshape(team * rows, qkv_cols + HEAD_SIZE)
    w_qkv = lay.weight_gather(packed).reshape(width, qkv_cols + HEAD_SIZE)

    w_rows = lay.weight_gather(jnp.concatenate([w_out, w_down]))
    by_column = lambda w: w.reshape(rows, teams, team, down_rows).transpose(2, 0, 1, 3).reshape(team, rows, ff)
    packed = jnp.concatenate([by_column(w_gate), by_column(w_up)], axis=2)
    packed = lay.exchange(packed).reshape(team * rows, 2 * ff)
    w_gate_up = lay.weight_gather(packed).reshape(width, 2 * ff)
    per = teams // team
    w_out_all = lay.exchange(w_rows[:, :out_rows].reshape(team, per * out_rows, width))
    w_out_all = (
        w_out_all.reshape(team, per, out_rows, width).transpose(1, 0, 2, 3).reshape(q_cols, width)
    )
    w_down_all = w_rows[:, out_rows:].reshape(ff, width)
    cot_own = to_halves(cotangent)
    cot_all = lay.team_gather(cot_own)

    gains = w_qkv[:, qkv_cols:].astype(F32)
    firsts = gains.reshape(devices, rows, HEAD_SIZE)[:, 0]
    gain_q = firsts[:, :few].reshape(1, HEAD_SIZE)
    gain_k = firsts[:, few : 2 * few].reshape(1, HEAD_SIZE)
    gain_one = gains[:, 2 * few].reshape(1, width)
    gain_two = gains[:, 2 * few + 1].reshape(1, width)

    cosine, sine = rope_tables(tokens)

    normed, raw, q, k, v = qkv_forward(
        x_all, gain_one, gain_q, gain_k, cosine, sine, w_qkv, queries, keys
    )
    attn, lse, part = attention_forward(prefix, q, k, v, w_out_all)
    xfloat = x_own.astype(F32)
    resid = xfloat + lay.team_scatter(part, span)
    scale_two = row_scale(resid)
    mlp_in = (resid * scale_two * gain_two).astype(BF16)
    mlp_all = lay.team_gather(mlp_in)
    hidden, gate_up_grad, out_part, mlp_part = mlp(mlp_all, cot_all, w_gate_up, w_down_all)

    mlp_grad = lay.team_scatter(mlp_part, span)
    resid_grad = cot_own.astype(F32) + norm_backward(resid, scale_two, gain_two, mlp_grad)
    out_grad = lay.team_gather(resid_grad.astype(BF16))
    dq, dk, dv = attention_backward(prefix, out_grad, w_out_all, q, k, v, lse)
    qkv_grad, back_part, gain_part = qkv_backward(
        dq, dk, dv, raw, gain_q, gain_k, cosine, sine, w_qkv, queries, keys
    )
    normed_grad = lay.team_scatter(back_part, span)
    input_part = norm_backward(xfloat, row_scale(xfloat), gain_one, normed_grad)

    def from_halves(value):
        got = swap(pick(value, 1 - lay.h).astype(BF16), "h").astype(value.dtype)
        return ordered(pick(value, lay.h), got, lay.h)

    output = from_halves((resid + lay.team_scatter(out_part, span)).astype(BF16))
    input_grad = from_halves(resid_grad + input_part)

    grad_down = lay.weight_scatter(dot_tn(hidden, cot_all).reshape(teams, down_rows, width))
    grad_gate_up = dot_tn(mlp_all, gate_up_grad).reshape(teams, team * rows, 2 * ff)
    grad_gate_up = lay.weight_scatter(grad_gate_up).astype(BF16).reshape(team, rows, 2 * ff)
    grad_gate_up = lay.exchange(grad_gate_up).astype(F32)
    back_column = lambda g: g.reshape(team, rows, teams, down_rows).transpose(1, 2, 0, 3).reshape(rows, -1)
    grad_gate = back_column(grad_gate_up[:, :, :ff])
    grad_up = back_column(grad_gate_up[:, :, ff:])
    grad_out = dot_tn(attn, out_grad).astype(BF16).reshape(per, team, out_rows, width)
    grad_out = lay.exchange(grad_out.transpose(1, 0, 2, 3).reshape(team, per * out_rows, width))
    grad_out = lay.weight_scatter(grad_out.astype(F32).reshape(teams, out_rows, width))

    gain_cols = jnp.concatenate(
        [gain_part[0].reshape(devices, 1, few), gain_part[1].reshape(devices, 1, few)], axis=2
    )
    gain_cols = jnp.pad(gain_cols, ((0, 0), (0, rows - 1), (0, HEAD_SIZE - 2 * few)))
    grad_qkv = jnp.concatenate([dot_tn(normed, qkv_grad), gain_cols.reshape(width, HEAD_SIZE)], axis=1)
    grad_qkv = lay.weight_scatter(grad_qkv.reshape(teams, team * rows, qkv_cols + HEAD_SIZE))
    grad_qkv = lay.exchange(grad_qkv.astype(BF16).reshape(team, rows, qkv_cols + HEAD_SIZE))
    grad_qkv = grad_qkv.astype(F32).transpose(1, 0, 2)
    grad_query = grad_qkv[:, :, :q_cols].reshape(rows, -1)
    grad_key = grad_qkv[:, :, q_cols : q_cols + k_cols].reshape(rows, -1)
    grad_value = grad_qkv[:, :, q_cols + k_cols : qkv_cols].reshape(rows, -1)
    small = jnp.sum(grad_qkv[0, :, qkv_cols : qkv_cols + 2 * few], axis=0)
    grad_gain_query, grad_gain_key = small[:few], small[few:]

    def gain_gradient(gain, pairs):
        total = sum(jnp.sum(w.astype(F32) * g, axis=1) for w, g in pairs)
        return total / gain.astype(F32)

    grad_gain_attn = gain_gradient(
        gain_attn, ((w_query, grad_query), (key_weight, grad_key), (value_weight, grad_value))
    )
    grad_gain_mlp = gain_gradient(gain_mlp, ((w_gate, grad_gate), (w_up, grad_up)))
    return (
        output, input_grad, grad_gain_attn, grad_query, grad_key, grad_value, grad_gain_query,
        grad_gain_key, grad_out, grad_gain_mlp, grad_gate, grad_up, grad_down,
    )


def solution(mesh):
    dp, ctx = mesh.shape["dp"], mesh.shape["ctx"]
    fine = Mesh(mesh.devices.reshape(2, dp // 2, 2, ctx // 4, 2), ("a", "b", "h", "l", "c"))
    tokens = P(("a", "b"), ("h", "l", "c"), None)
    sequences = P(("a", "b"))
    vector = P(("a", "b", "h", "l", "c"))
    matrix = P(("a", "b", "h", "l", "c"), None)
    return jax.shard_map(
        per_device,
        mesh=fine,
        in_specs=(
            tokens, sequences, vector, matrix, matrix, matrix, vector, vector, matrix, vector,
            matrix, matrix, matrix, tokens,
        ),
        out_specs=(
            tokens, tokens, vector, matrix, matrix, matrix, vector, vector, matrix, vector,
            matrix, matrix, matrix,
        ),
        check_vma=False,
    )
```
